256 devices in a mesh: expert: 16 (over y, z_lo), batch: 16 (over x, z_hi, core).
Axes of the slice: x: 4, y: 4, z: 8 (z_hi: 2, z_lo: 4; z = z_hi * 4 + z_lo), core: 2. Of those that a mesh axis runs over, the one named last changes fastest.
Arguments:
- tokens: bfloat16 [16, 1024, 7168], P('expert', 'batch'), may hold values from -6 to 6
- route_prob: float32 [16, 1024], P('expert', 'batch'), may hold values from 0.2 to 1
- counts: int32 [16, 16], replicated, may hold values from 1 to 32, as said below
- w_gate: bfloat16 [16, 7168, 2048], P('expert', None, 'batch'), may hold values from -0.0625 to 0.0625
- w_up: bfloat16 [16, 7168, 2048], P('expert', None, 'batch'), may hold values from -0.0625 to 0.0625
- w_down: bfloat16 [16, 2048, 7168], P('expert', 'batch'), may hold values from -0.125 to 0.125
Outputs:
- returned: bfloat16 [16, 1024, 7168], P('expert', 'batch')
The draws below stay inside these ranges and needn't reach their ends.
Inputs may be any that keep to these rules, and one draw needn't show every extreme that they name: Live slot counts of the blocks, at most 32; some block has exactly 32 in every draw, and experts differ in load.
All inputs are finite; a program needn't handle non-finite values.
Results may differ from the reference program's by a relative error of at most 0.014.
Values may be sent and summed in bfloat16 or wider, within the bound.
A program may use at most 128 MiB of HBM per device.

```python
import jax
import jax.numpy as jnp
from jax import lax

D = 7168
FF = 2048
CAP = 64
LIVE = 32
E = 16
BTOK = 1024
SLOT = 4
N_BATCH = 16


def draw_counts(key, part):
    keys = jax.random.split(key, 4)
    heat = jax.random.randint(keys[0], (E, 1), 1, 5)
    base = jax.random.randint(keys[1], (E, N_BATCH), max(CAP // 16, 1), CAP // 8 + 1)
    loads = jnp.clip(base * heat, 1, LIVE)
    first = jax.random.randint(keys[2], (), 0, E)
    second = jax.random.randint(keys[3], (), 0, N_BATCH)
    loads = loads.at[first, second].set(LIVE)
    return loads.astype(jnp.int32)


def block_scale(own_key, extent, shards, low, top_value):
    level = 1.0
    for position, blocks in shards:
        steps = jax.random.uniform(jax.random.fold_in(jax.random.fold_in(own_key, 6), position), (blocks,), jnp.float32, low / len(shards), top_value / len(shards))
        level = level * jnp.repeat(jnp.exp(steps), extent[position] // blocks).reshape((-1,) + (1,) * (len(extent) - 1 - position))
    return level


def noise(stream_key, extent, spread, limit, shards=(), kind=jnp.bfloat16):
    gain = block_scale(stream_key, extent, shards, -0.22, 0.18) if shards else 1.0
    result = jax.random.normal(stream_key, extent, jnp.float32) * spread * gain
    return jnp.minimum(jnp.maximum(result, -limit), limit).astype(kind)


def setup_inputs(seed: int = 0) -> dict:
    key_of = jax.random.split(jax.random.key(seed), 7)
    tokens = noise(key_of[0], (E, BTOK, D), 1.0, 6.0, ((0, 16), (1, 16)))
    route_prob = jnp.clip(0.2 + 0.8 * jax.random.uniform(key_of[1], (E, BTOK), jnp.float32) ** block_scale(key_of[1], (E, BTOK), ((0, 16), (1, 16)), -0.2, 0.2), 0.2, 1.0)
    counts = draw_counts(jax.random.fold_in(key_of[6], 71), 0)
    w_gate = noise(key_of[3], (E, D, FF), D ** -0.5, 0.0625, ((0, 16), (2, 16)))
    w_up = noise(key_of[4], (E, D, FF), D ** -0.5, 0.0625, ((0, 16), (2, 16)))
    w_down = noise(key_of[5], (E, FF, D), FF ** -0.5, 0.125, ((0, 16), (1, 16)))
    return {"tokens": tokens, "route_prob": route_prob, "counts": counts, "w_gate": w_gate, "w_up": w_up, "w_down": w_down}


def one_expert(operands):
    inputs, weights_prob, live_counts, gate_w, up_w, down_w = operands
    gate = jnp.dot(inputs, gate_w, preferred_element_type=jnp.float32)
    upper = jnp.dot(inputs, up_w, preferred_element_type=jnp.float32)
    hidden = (jax.nn.silu(gate) * upper).astype(jnp.bfloat16)
    group = FF // N_BATCH
    hidden_parts = hidden.reshape(BTOK, N_BATCH, group).transpose(1, 0, 2)
    down_parts = down_w.reshape(N_BATCH, group, D)

    def add_part(total, pair):
        hidden_piece, down_piece = pair
        partial_value = jnp.dot(hidden_piece, down_piece, preferred_element_type=jnp.float32).astype(jnp.bfloat16)
        partial_value = lax.optimization_barrier(partial_value)
        return total + partial_value.astype(jnp.float32), None

    summed, _ = lax.scan(add_part, jnp.zeros((BTOK, D), jnp.float32), (hidden_parts, down_parts))
    slots = jnp.arange(CAP, dtype=jnp.int32)
    live = (slots[None, :] < live_counts[:, None]).reshape(BTOK)
    scaled = weights_prob[:, None] * summed
    return jnp.where(live[:, None], scaled, 0.0).astype(jnp.bfloat16)


def reference(tokens, route_prob, counts, w_gate, w_up, w_down):
    expert_out = lax.map(one_expert, (tokens, route_prob, counts, w_gate, w_up, w_down))
    blocks = expert_out.reshape(E, N_BATCH, E, SLOT, D)
    return blocks.transpose(2, 1, 0, 3, 4).reshape(E, BTOK, D)
```

```python
import functools

import jax
import jax.numpy as jnp
from jax import lax
from jax.experimental import pallas as pl
from jax.experimental.pallas import tpu as pltpu
from jax.sharding import PartitionSpec as P

MESH = pl.DeviceIdType.MESH
BF = jnp.bfloat16
F32 = jnp.float32

D = 7168
FF1 = 128
LIVE = 32
PL = 8
COLS = D // PL
ROWS = PL * LIVE
KSTEP = 1024


def kernel(counts, prob, tok, wg, wu, wdn, out, wgu, wd, tok_p, tok_o, hid_p, hid_o, zs, zr, fs, oacc, sc, acc, zero, ss, rs, ls, fss, fsr, fs0, zsem):
    div, rem = lax.div, lax.rem
    e = lax.axis_index("expert")
    b = lax.axis_index("batch")
    x = div(b, 4)
    h = rem(div(b, 2), 2)
    c = rem(b, 2)
    k = x * 2 + c
    xr, x2, xl = rem(x + 1, 4), rem(x + 2, 4), rem(x + 3, 4)
    lo, hi = pl.ds(0, 16), pl.ds(16, 16)

    def dev(x_, h_, c_):
        return (e, x_ * 4 + h_ * 2 + c_)

    def member(kk):
        return div(kk, 2) * 4 + h * 2 + rem(kk, 2)

    right, left, across = dev(xr, h, c), dev(xl, h, c), dev(x2, h, c)
    core, zmate = dev(x, h, 1 - c), dev(x, 1 - h, c)
    slot_r, slot_2, slot_l = xr * 2 + c, x2 * 2 + c, xl * 2 + c

    loads = [
        pltpu.make_async_copy(wg.at[0], wgu.at[:, pl.ds(0, FF1)], ls.at[0]),
        pltpu.make_async_copy(wu.at[0], wgu.at[:, pl.ds(FF1, FF1)], ls.at[1]),
        pltpu.make_async_copy(
            wdn.at[0, :, pl.ds(pl.multiple_of(k * COLS, 128), COLS)],
            wd.at[pl.ds(pl.multiple_of(k * FF1, FF1), FF1)], ls.at[2]),
        pltpu.make_async_copy(tok.at[0, pl.ds(0, LIVE)], tok_o.at[k], ls.at[3]),
    ]
    for cp in loads:
        cp.start()

    bar = pltpu.get_barrier_semaphore()
    for dx in range(4):
        for dc in range(2):
            if dx or dc:
                pl.semaphore_signal(bar, inc=1, device_id=dev(rem(x + dx, 4), h, rem(c + dc, 2)), device_id_type=MESH)
    pl.semaphore_signal(bar, inc=1, device_id=zmate, device_id_type=MESH)

    @pl.when(e < 8)
    def _():
        for t in range(16):
            for d in range(PL):
                pl.semaphore_signal(bar, inc=1, device_id=(rem(e + t, 16), member(rem(k + d, PL))), device_id_type=MESH)

    own = counts[e, b]
    for r in range(LIVE):
        value = jnp.where(r < own, prob[0, r], 0.0)
        sc[k, pl.ds(r, 1), :] = jnp.full((1, 128), value, F32)

    @pl.when(e >= 8)
    def _():
        zero[...] = jnp.zeros_like(zero)
        for i in range(16):
            pltpu.make_async_copy(zero, out.at[i], zsem).start()
        pltpu.make_async_copy(out, out, zsem).wait()

    pl.semaphore_wait(bar, PL + 64)

    sends = []

    def send(src, dst, to):
        i = len(sends)
        cp = pltpu.make_async_remote_copy(src, dst, ss.at[i], rs.at[i], device_id=to, device_id_type=MESH)
        cp.start()
        sends.append(cp)
        return cp

    z_lo = send(tok.at[0, lo], tok_p.at[k, lo], zmate)
    z_hi = send(tok.at[0, hi], tok_p.at[k, hi], zmate)
    o_core = [send(tok.at[0, pl.ds(0, LIVE)], tok_o.at[k], core)]
    wcp, scp = [], []
    for dx, dc in ((0, 1), (1, 0), (3, 0), (2, 0), (1, 1), (3, 1), (2, 1)):
        x_, c_ = rem(x + dx, 4), rem(c + dc, 2)
        kk = x_ * 2 + c_
        wcp.append(send(
            wdn.at[0, :, pl.ds(pl.multiple_of(kk * COLS, 128), COLS)],
            wd.at[pl.ds(pl.multiple_of(k * FF1, FF1), FF1)], dev(x_, h, c_)))
    for dx, dc in ((0, 1), (1, 0), (3, 0), (2, 0), (1, 1), (3, 1), (2, 1)):
        scp.append(send(sc.at[k], sc.at[k], dev(rem(x + dx, 4), h, rem(c + dc, 2))))

    z_lo.wait_recv()
    p_ar = send(tok_p.at[k, lo], tok_p.at[k, lo], right)
    p_al = send(tok_p.at[k, lo], tok_p.at[k, lo], left)
    z_hi.wait_recv()
    p_bl = send(tok_p.at[k, hi], tok_p.at[k, hi], left)
    p_br = send(tok_p.at[k, hi], tok_p.at[k, hi], right)
    p_core = [send(tok_p.at[k], tok_p.at[k], core)]
    p_ar.wait_recv()
    p_fa = send(tok_p.at[slot_l, lo], tok_p.at[slot_l, lo], right)
    p_bl.wait_recv()
    p_fb = send(tok_p.at[slot_r, hi], tok_p.at[slot_r, hi], left)
    loads[3].wait()
    o_ar = send(tok_o.at[k, lo], tok_o.at[k, lo], right)
    o_bl = send(tok_o.at[k, hi], tok_o.at[k, hi], left)
    p_br.wait_recv()
    p_core.append(send(tok_p.at[slot_l], tok_p.at[slot_l], core))
    p_al.wait_recv()
    p_core.append(send(tok_p.at[slot_r], tok_p.at[slot_r], core))
    p_fa.wait_recv()
    p_fb.wait_recv()
    p_core.append(send(tok_p.at[slot_2], tok_p.at[slot_2], core))
    for cp in p_core:
        cp.wait_recv()
    loads[0].wait()
    loads[1].wait()

    def gate_up(tk, hid):
        acc[...] = jnp.zeros_like(acc)

        def step(i, _):
            cols = pl.ds(pl.multiple_of(i * KSTEP, KSTEP), KSTEP)
            acc[...] += jnp.dot(tk[:, :, cols].reshape(ROWS, KSTEP), wgu[cols, :], preferred_element_type=F32)
            return 0

        lax.fori_loop(0, D // KSTEP, step, 0)
        gate = acc[:, :FF1]
        hid[:, pl.ds(pl.multiple_of(k * FF1, FF1), FF1)] = (gate / (1.0 + jnp.exp(-gate)) * acc[:, FF1:]).astype(BF)

    def hid_cols(ref, kk):
        return ref.at[:, pl.ds(pl.multiple_of(kk * FF1, FF1), FF1)]

    def spread_hidden(hid):
        mine = hid_cols(hid, k)
        lane = [(send(mine, mine, to), hid_cols(hid, s)) for to, s in ((right, slot_l), (left, slot_r), (across, slot_2))]
        return lane, [send(mine, mine, core)]

    def collect_hidden(lane, from_core):
        for cp, part in lane:
            cp.wait_recv()
            from_core.append(send(part, part, core))
        for cp in from_core:
            cp.wait_recv()

    def down(hid, store):
        def step(j, _):
            cols = pl.ds(pl.multiple_of(j * 128, 128), 128)
            store(cols, jnp.dot(hid[...], wd[:, cols], preferred_element_type=F32))
            return 0

        lax.fori_loop(0, COLS // 128, step, 0)

    gate_up(tok_p, hid_p)
    p_lane, p_hcore = spread_hidden(hid_p)
    o_br = send(tok_o.at[k, hi], tok_o.at[k, hi], right)
    o_al = send(tok_o.at[k, lo], tok_o.at[k, lo], left)
    o_ar.wait_recv()
    o_fa = send(tok_o.at[slot_l, lo], tok_o.at[slot_l, lo], right)
    o_bl.wait_recv()
    o_fb = send(tok_o.at[slot_r, hi], tok_o.at[slot_r, hi], left)
    collect_hidden(p_lane, p_hcore)
    loads[2].wait()
    for cp in wcp:
        cp.wait_recv()

    def store_p(cols, value):
        zs[:, :, cols] = value.astype(BF).reshape(PL, LIVE, 128)

    down(hid_p, store_p)
    zcp = []
    for d in range(PL):
        kk = rem(k + d, PL)
        zcp.append(send(zs.at[kk], zr.at[kk], zmate))

    o_br.wait_recv()
    o_core.append(send(tok_o.at[slot_l], tok_o.at[slot_l], core))
    o_al.wait_recv()
    o_core.append(send(tok_o.at[slot_r], tok_o.at[slot_r], core))
    o_fa.wait_recv()
    o_fb.wait_recv()
    o_core.append(send(tok_o.at[slot_2], tok_o.at[slot_2], core))
    for cp in o_core:
        cp.wait_recv()
    gate_up(tok_o, hid_o)
    o_lane, o_hcore = spread_hidden(hid_o)
    collect_hidden(o_lane, o_hcore)

    def store_o(cols, value):
        oacc[:, :, cols] = value.reshape(PL, LIVE, 128)

    down(hid_o, store_o)
    for cp in scp:
        cp.wait_recv()

    mycols = pl.ds(pl.multiple_of(k * COLS, 128), COLS)
    for d in range(PL):
        kk = rem(k + d, PL)
        zcp[d].wait_recv()
        scale = sc[kk]
        for j in range(COLS // 128):
            cols = pl.ds(j * 128, 128)
            total = (oacc[kk, :, cols] + zr[kk, :, cols].astype(F32)) * scale
            total = jnp.where(scale > 0.0, total, 0.0)
            fs[kk, :, :, cols] = total.reshape(8, 4, 128).astype(BF)
        for t in range(8):
            s = rem(e + t, 8)
            src, dst = fs.at[kk, s], out.at[e, :, mycols]
            sem = fs0 if d == 0 and t == 0 else fss.at[d]
            remote = pltpu.make_async_remote_copy(src, dst, sem, fsr, device_id=(s, member(kk)), device_id_type=MESH)
            if d == 0 and t == 0:
                pl.when(e >= 8)(remote.start)
                pl.when(e < 8)(pltpu.make_async_copy(src, dst, fsr).start)
            else:
                remote.start()

    for cp in sends:
        cp.wait_send()
    for d in range(PL):
        part = fs.at[d, pl.ds(0, 7 if d == 0 else 8)]
        pltpu.make_async_copy(part, part, fss.at[d]).wait()

    @pl.when(e >= 8)
    def _():
        pltpu.make_async_copy(fs.at[0, 0], fs.at[0, 0], fs0).wait()

    @pl.when(e < 8)
    def _():
        pltpu.make_async_copy(out, out, fsr).wait()


def body(tokens, route_prob, counts, w_gate, w_up, w_down):
    any_ = pl.BlockSpec(memory_space=pl.ANY)
    smem = pl.BlockSpec(memory_space=pltpu.SMEM)
    out = pl.pallas_call(
        kernel,
        name="routed_experts",
        out_shape=jax.ShapeDtypeStruct((16, 4, D), BF),
        in_specs=[smem, smem, any_, any_, any_, any_],
        out_specs=any_,
        scratch_shapes=[
            pltpu.VMEM((D, 2 * FF1), BF),
            pltpu.VMEM((PL * FF1, COLS), BF),
            pltpu.VMEM((PL, LIVE, D), BF),
            pltpu.VMEM((PL, LIVE, D), BF),
            pltpu.VMEM((ROWS, PL * FF1), BF),
            pltpu.VMEM((ROWS, PL * FF1), BF),
            pltpu.VMEM((PL, LIVE, COLS), BF),
            pltpu.VMEM((PL, LIVE, COLS), BF),
            pltpu.VMEM((PL, 8, 4, COLS), BF),
            pltpu.VMEM((PL, LIVE, COLS), F32),
            pltpu.VMEM((PL, LIVE, 128), F32),
            pltpu.VMEM((ROWS, 2 * FF1), F32),
            pltpu.VMEM((4, D), BF),
            pltpu.SemaphoreType.DMA((80,)),
            pltpu.SemaphoreType.DMA((80,)),
            pltpu.SemaphoreType.DMA((4,)),
            pltpu.SemaphoreType.DMA((PL,)),
            pltpu.SemaphoreType.DMA,
            pltpu.SemaphoreType.DMA,
            pltpu.SemaphoreType.DMA,
        ],
        compiler_params=pltpu.CompilerParams(
            collective_id=0, has_side_effects=True, vmem_limit_bytes=60 * 1024 * 1024),
    )(counts, route_prob, tokens, w_gate, w_up, w_down)
    return out.reshape(1, 64, D)


def solution(mesh):
    in_specs = (
        P("expert", "batch", None),
        P("expert", "batch"),
        P(),
        P("expert", None, "batch"),
        P("expert", None, "batch"),
        P("expert", "batch", None),
    )
    out_specs = P("expert", "batch", None)
    return jax.shard_map(body, mesh=mesh, in_specs=in_specs, out_specs=out_specs, check_vma=False)
```

```python
import jax
import jax.numpy as jnp
from jax import lax
from jax.experimental import pallas as pl
from jax.experimental.pallas import tpu as pltpu
from jax.sharding import PartitionSpec as P

MESH = pl.DeviceIdType.MESH
BF = jnp.bfloat16
F32 = jnp.float32

D = 7168
HALF = D // 2
FF1 = 128
PL = 8
COLS = D // PL
HR = 16
ROWS = PL * HR
KSTEP = 1024


def kernel(counts, prob, tok, wg, wu, wdn, out, wgu, wd, raw, tks, hid, zs, zr, oacc, fs, pr, sc, acc, zero, ss, rs, bs, ls, fss, fsr, fs0, zsem):
    div, rem = lax.div, lax.rem
    e = lax.axis_index("expert")
    b = lax.axis_index("batch")
    x, h, c = div(b, 4), rem(div(b, 2), 2), rem(b, 2)
    k = x * 2 + c
    xr, x2, xl = rem(x + 1, 4), rem(x + 2, 4), rem(x + 3, 4)

    def dev(x_, h_, c_, e_=e):
        return (e_, x_ * 4 + h_ * 2 + c_)

    def mate(d):
        kk = rem(k + d, PL)
        return kk, div(kk, 2), rem(kk, 2)

    right, left, across = dev(xr, h, c), dev(xl, h, c), dev(x2, h, c)
    core, zmate = dev(x, h, 1 - c), dev(x, 1 - h, c)
    slot_r, slot_2, slot_l = xr * 2 + c, x2 * 2 + c, xl * 2 + c

    def cols_of(kk, width):
        return pl.ds(pl.multiple_of(kk * width, 128), width)

    loads = [
        pltpu.make_async_copy(tok.at[0, pl.ds(0, 2 * HR)], raw, ls.at[3]),
        pltpu.make_async_copy(wg.at[0], wgu.at[:, pl.ds(0, FF1)], ls.at[0]),
        pltpu.make_async_copy(wu.at[0], wgu.at[:, pl.ds(FF1, FF1)], ls.at[1]),
        pltpu.make_async_copy(wdn.at[0, :, cols_of(k, COLS)], wd.at[cols_of(k, FF1)], ls.at[2]),
    ]
    for cp in loads:
        cp.start()

    bar = pltpu.get_barrier_semaphore()

    def greet(to):
        pl.semaphore_signal(bar, inc=1, device_id=to, device_id_type=MESH)

    for d in range(1, PL):
        _, x_, c_ = mate(d)
        greet(dev(x_, h, c_))
    greet(zmate)

    @pl.when(e < 8)
    def _():
        for t in range(16):
            for d in range(PL):
                _, x_, c_ = mate(d)
                greet(dev(x_, h, c_, rem(e + t, 16)))

    loads[0].wait()
    new = lax.broadcasted_iota(jnp.int32, (2 * HR, 2 * HR), 0)
    old = lax.broadcasted_iota(jnp.int32, (2 * HR, 2 * HR), 1)
    source = 4 * div(rem(new, HR), 2) + 2 * div(new, HR) + rem(new, 2)
    order = jnp.where(source == old, 1.0, 0.0).astype(BF)

    def reorder(i, _):
        cols = pl.ds(pl.multiple_of(i * KSTEP, KSTEP), KSTEP)
        value = jnp.dot(order, raw[:, cols], preferred_element_type=F32).astype(BF)
        tks[0, 0, k, :, cols] = value[:HR]
        tks[0, 1, k, :, cols] = value[HR:]
        return 0

    lax.fori_loop(0, D // KSTEP, reorder, 0)

    own = counts[e, b]
    slots = lax.broadcasted_iota(jnp.int32, (1, 64), 1)
    pr[k] = jnp.zeros((1, 128), F32)
    pr[k, :, pl.ds(0, 64)] = jnp.where(slots < own, prob[...], 0.0)

    pl.semaphore_wait(bar, PL + 64)

    count = []

    def send(src, dst, to, sent, got=None):
        if got is None:
            here = rs.at[len(count)]
            count.append(0)
        else:
            here = bs.at[got]
        cp = pltpu.make_async_remote_copy(src, dst, ss.at[sent], here, device_id=to, device_id_type=MESH)
        cp.start()
        return cp

    def take(part, sem):
        pltpu.make_async_copy(part, part, sem).wait()

    zcp = [send(tks.at[0, q, k], tks.at[1, q, k], zmate, 2) for q in range(2)]
    for q in range(2):
        send(tks.at[0, q, k], tks.at[0, q, k], core, 3 + q, 2 + q)
    scp = []
    for d in range(1, PL):
        _, x_, c_ = mate(d)
        scp.append(send(pr.at[k], pr.at[k], dev(x_, h, c_), 1, 1))
    for dx, dc in ((0, 1), (1, 0), (3, 0), (2, 0), (1, 1), (3, 1), (2, 1)):
        x_, c_ = rem(x + dx, 4), rem(c + dc, 2)
        send(wdn.at[0, :, cols_of(x_ * 2 + c_, COLS)], wd.at[cols_of(k, FF1)], dev(x_, h, c_), 0, 0)

    col0, col1 = pl.ds(0, HALF), pl.ds(HALF, HALF)

    class Chunk:
        def __init__(self, plane, q):
            self.plane, self.q = plane, q
            self.t = tks.at[plane, q]

        def piece(self, slot, cols, to, got=None):
            part = self.t.at[slot, :, cols]
            return send(part, part, to, 3 + self.plane * 2 + self.q, got)

        def to_core(self, slot, cols):
            self.piece(slot, cols, core, 2 + self.plane * 2 + self.q)

        def first(self):
            if self.plane == 1:
                zcp[self.q].wait_recv()
            self.r0 = self.piece(k, col0, right)
            self.l1 = self.piece(k, col1, left)
            self.r1 = self.piece(k, col1, right)
            self.l0 = self.piece(k, col0, left)
            if self.plane == 1:
                self.to_core(k, pl.ds(0, D))

        def second(self):
            self.r0.wait_recv()
            self.f0 = self.piece(slot_l, col0, right)
            self.l1.wait_recv()
            self.f1 = self.piece(slot_r, col1, left)
            self.to_core(slot_l, col0)
            self.to_core(slot_r, col1)

        def finish(self):
            for cp, slot, cols in ((self.r1, slot_l, col1), (self.l0, slot_r, col0), (self.f0, slot_2, col0), (self.f1, slot_2, col1)):
                cp.wait_recv()
                self.to_core(slot, cols)
            take(self.t.at[pl.ds(0, 4)], bs.at[2 + self.plane * 2 + self.q])

        def gate_up(self):
            tk = self.t
            self.hid = hid.at[self.plane * 2 + self.q]
            acc[...] = jnp.zeros_like(acc)

            def step(i, _):
                cols = pl.ds(pl.multiple_of(i * KSTEP, KSTEP), KSTEP)
                acc[...] += jnp.dot(tk[:, :, cols].reshape(ROWS, KSTEP), wgu[cols, :], preferred_element_type=F32)
                return 0

            lax.fori_loop(0, D // KSTEP, step, 0)
            gate = acc[:, :FF1]
            self.hid[:, cols_of(k, FF1)] = (gate / (1.0 + jnp.exp(-gate)) * acc[:, FF1:]).astype(BF)
            mine = self.hid.at[:, cols_of(k, FF1)]
            n = self.plane * 2 + self.q
            self.lane = [(send(mine, mine, to, 7 + n), slot) for to, slot in ((across, slot_2), (right, slot_l), (left, slot_r))]
            send(mine, mine, core, 7 + n, 6 + n)

        def collect(self):
            n = self.plane * 2 + self.q
            for cp, slot in self.lane[1:] + self.lane[:1]:
                cp.wait_recv()
                part = self.hid.at[:, cols_of(slot, FF1)]
                send(part, part, core, 7 + n, 6 + n)
            take(self.hid.at[:, pl.ds(0, 4 * FF1)], bs.at[6 + n])

        def down(self):
            for start, width in ((0, 256), (256, 256), (512, 256), (768, 128)):
                cols = pl.ds(start, width)
                value = jnp.dot(self.hid[...], wd[:, cols], preferred_element_type=F32).reshape(PL, HR, width)
                if self.plane == 1:
                    zs[self.q, :, :, cols] = value.astype(BF)
                else:
                    oacc[self.q, :, :, cols] = value
            if self.plane == 1:
                self.z = []
                for d in range(PL):
                    kk, _, _ = mate(d)
                    self.z.append(send(zs.at[self.q, kk], zr.at[self.q, kk], zmate, 11 + self.q))

    mycols = cols_of(k, COLS)

    def last_hop(q, ch):
        for d in range(PL):
            kk, x_, c_ = mate(d)
            ch.z[d].wait_recv()
            scale = sc[kk, pl.ds(q * HR, HR), :]
            for j in range(0, COLS, 128):
                cols = pl.ds(j, 128)
                total = (oacc[q, kk, :, cols] + zr[q, kk, :, cols].astype(F32)) * scale
                total = jnp.where(scale > 0.0, total, 0.0)
                fs[q, kk, :, :, cols] = total.reshape(8, 2, 128).astype(BF)
            for t in range(8):
                s = rem(e + t, 8)
                src, dst = fs.at[q, kk, s], out.at[e, q, :, mycols]
                sem = fss.at[q, 0] if d else fs0.at[q] if t == 0 else fss.at[q, 1]
                remote = pltpu.make_async_remote_copy(src, dst, sem, fsr, device_id=dev(x_, h, c_, s), device_id_type=MESH)
                if d == 0 and t == 0:
                    pl.when(e >= 8)(remote.start)
                    pl.when(e < 8)(pltpu.make_async_copy(src, dst, fsr).start)
                else:
                    remote.start()

    p0, p1, o0, o1 = Chunk(1, 0), Chunk(1, 1), Chunk(0, 0), Chunk(0, 1)
    @pl.when(e >= 8)
    def _():
        zero[...] = jnp.zeros_like(zero)
        for i in range(16):
            pltpu.make_async_copy(zero, out.at[i], zsem).start()

    p0.first()
    p0.second()
    p1.first()
    loads[1].wait()
    loads[2].wait()
    p0.finish()
    p0.gate_up()
    p1.second()

    take(pr.at[pl.ds(0, 7)], bs.at[1])
    slot_i = lax.broadcasted_iota(jnp.int32, (2 * HR, 128), 1)
    row_i = lax.broadcasted_iota(jnp.int32, (2 * HR, 128), 0)
    from_i = 4 * div(rem(row_i, HR), 2) + 2 * div(row_i, HR) + rem(row_i, 2)
    for kk in range(PL):
        column = jnp.sum(jnp.where(slot_i == from_i, pr[kk], 0.0), axis=1, keepdims=True)
        sc[kk] = jnp.broadcast_to(column, (2 * HR, 128))
    o0.first()
    p0.collect()
    loads[3].wait()
    take(wd.at[pl.ds(0, 7 * FF1)], bs.at[0])
    p0.down()
    p1.finish()
    p1.gate_up()
    o0.second()
    o1.first()
    p1.collect()
    p1.down()
    o0.finish()
    o0.gate_up()
    o1.second()
    o0.collect()
    o0.down()
    o1.finish()
    o1.gate_up()
    last_hop(0, p0)
    o1.collect()
    o1.down()
    last_hop(1, p1)

    take(wd.at[pl.ds(0, 7 * FF1)], ss.at[0])
    take(pr.at[pl.ds(0, 7)], ss.at[1])
    take(tks.at[0, 0, pl.ds(0, 2)], ss.at[2])
    for n in range(4):
        take(tks.at[0, 0, pl.ds(0, 7)], ss.at[3 + n])
        take(hid.at[0, :, pl.ds(0, 7 * FF1)], ss.at[7 + n])
    for q in range(2):
        take(zs.at[q], ss.at[11 + q])
    for q in range(2):
        take(fs.at[q, pl.ds(0, PL - 1)], fss.at[q, 0])
        take(fs.at[q, 0, pl.ds(0, 7)], fss.at[q, 1])

        @pl.when(e >= 8)
        def _():
            take(fs.at[q, 0, 0], fs0.at[q])

    @pl.when(e >= 8)
    def _():
        take(out, zsem)

    @pl.when(e < 8)
    def _():
        take(out, fsr)


def body(tokens, route_prob, counts, w_gate, w_up, w_down):
    any_ = pl.BlockSpec(memory_space=pl.ANY)
    smem = pl.BlockSpec(memory_space=pltpu.SMEM)
    out = pl.pallas_call(
        kernel,
        name="routed_experts",
        out_shape=jax.ShapeDtypeStruct((16, 2, 2, D), BF),
        in_specs=[smem, pl.BlockSpec(memory_space=pltpu.VMEM), any_, any_, any_, any_],
        out_specs=any_,
        scratch_shapes=[
            pltpu.VMEM((D, 2 * FF1), BF),
            pltpu.VMEM((PL * FF1, COLS), BF),
            pltpu.VMEM((2 * HR, D), BF),
            pltpu.VMEM((2, 2, PL, HR, D), BF),
            pltpu.VMEM((4, ROWS, PL * FF1), BF),
            pltpu.VMEM((2, PL, HR, COLS), BF),
            pltpu.VMEM((2, PL, HR, COLS), BF),
            pltpu.VMEM((2, PL, HR, COLS), F32),
            pltpu.VMEM((2, PL, 8, 2, COLS), BF),
            pltpu.VMEM((PL, 1, 128), F32),
            pltpu.VMEM((PL, 2 * HR, 128), F32),
            pltpu.VMEM((ROWS, 2 * FF1), F32),
            pltpu.VMEM((2, 2, D), BF),
            pltpu.SemaphoreType.DMA((13,)),
            pltpu.SemaphoreType.DMA((54,)),
            pltpu.SemaphoreType.DMA((10,)),
            pltpu.SemaphoreType.DMA((4,)),
            pltpu.SemaphoreType.DMA((2, 2)),
            pltpu.SemaphoreType.DMA,
            pltpu.SemaphoreType.DMA((2,)),
            pltpu.SemaphoreType.DMA,
        ],
        compiler_params=pltpu.CompilerParams(
            collective_id=0, has_side_effects=True, vmem_limit_bytes=60 * 1024 * 1024),
    )(counts, route_prob, tokens, w_gate, w_up, w_down)
    return out.reshape(1, 64, D)


def solution(mesh):
    in_specs = (
        P("expert", "batch", None),
        P("expert", "batch"),
        P(),
        P("expert", None, "batch"),
        P("expert", None, "batch"),
        P("expert", "batch", None),
    )
    out_specs = P("expert", "batch", None)
    return jax.shard_map(body, mesh=mesh, in_specs=in_specs, out_specs=out_specs, check_vma=False)
```

```python
import jax
import jax.numpy as jnp
from jax import lax
from jax.experimental import pallas as pl
from jax.experimental.pallas import tpu as pltpu
from jax.sharding import PartitionSpec as P

MESH = pl.DeviceIdType.MESH
BF = jnp.bfloat16
F32 = jnp.float32

D = 7168
HALF = D // 2
FF1 = 128
PL = 8
COLS = D // PL
HR = 16
ROWS = PL * HR
KSTEP = 1024


def kernel(counts, prob, tok, wg, wu, wdn, out, wgu, wd, raw, tks, hid, zs, zr, oacc, fs, pr, sc, zero, ss, rs, bs, ls, fss, fsr, fs0, zsem):
    div, rem = lax.div, lax.rem
    e = lax.axis_index("expert")
    b = lax.axis_index("batch")
    x, h, c = div(b, 4), rem(div(b, 2), 2), rem(b, 2)
    k = x * 2 + c
    xr, x2, xl = rem(x + 1, 4), rem(x + 2, 4), rem(x + 3, 4)

    def dev(x_, h_, c_, e_=e):
        return (e_, x_ * 4 + h_ * 2 + c_)

    def mate(d):
        kk = rem(k + d, PL)
        return kk, div(kk, 2), rem(kk, 2)

    right, left, across = dev(xr, h, c), dev(xl, h, c), dev(x2, h, c)
    core, zmate = dev(x, h, 1 - c), dev(x, 1 - h, c)
    slot_r, slot_2, slot_l = xr * 2 + c, x2 * 2 + c, xl * 2 + c

    def cols_of(kk, width):
        return pl.ds(pl.multiple_of(kk * width, 128), width)

    loads = [
        pltpu.make_async_copy(tok.at[0, pl.ds(0, 2 * HR)], raw, ls.at[3]),
        pltpu.make_async_copy(wg.at[0], wgu.at[:, pl.ds(0, FF1)], ls.at[0]),
        pltpu.make_async_copy(wu.at[0], wgu.at[:, pl.ds(FF1, FF1)], ls.at[1]),
        pltpu.make_async_copy(wdn.at[0, :, cols_of(k, COLS)], wd.at[cols_of(k, FF1)], ls.at[2]),
    ]
    for cp in loads:
        cp.start()

    bar = pltpu.get_barrier_semaphore()

    def greet(to):
        pl.semaphore_signal(bar, inc=1, device_id=to, device_id_type=MESH)

    for d in range(1, PL):
        _, x_, c_ = mate(d)
        greet(dev(x_, h, c_))
    greet(zmate)

    @pl.when(e < 8)
    def _():
        for t in range(16):
            for d in range(PL):
                _, x_, c_ = mate(d)
                greet(dev(x_, h, c_, rem(e + t, 16)))

    loads[0].wait()
    new = lax.broadcasted_iota(jnp.int32, (2 * HR, 2 * HR), 0)
    old = lax.broadcasted_iota(jnp.int32, (2 * HR, 2 * HR), 1)
    source = 4 * div(rem(new, HR), 2) + 2 * div(new, HR) + rem(new, 2)
    order = jnp.where(source == old, 1.0, 0.0).astype(BF)

    def reorder(i, _):
        cols = pl.ds(pl.multiple_of(i * KSTEP, KSTEP), KSTEP)
        value = jnp.dot(order, raw[:, cols], preferred_element_type=F32).astype(BF)
        tks[0, 0, k, :, cols] = value[:HR]
        tks[0, 1, k, :, cols] = value[HR:]
        return 0

    lax.fori_loop(0, D // KSTEP, reorder, 0)

    own = counts[e, b]
    slots = lax.broadcasted_iota(jnp.int32, (1, 64), 1)
    pr[k] = jnp.zeros((1, 128), F32)
    pr[k, :, pl.ds(0, 64)] = jnp.where(slots < own, prob[...], 0.0)

    pl.semaphore_wait(bar, PL + 64)

    count = []

    def send(src, dst, to, sent, got=None):
        if got is None:
            here = rs.at[len(count)]
            count.append(0)
        else:
            here = bs.at[got]
        cp = pltpu.make_async_remote_copy(src, dst, ss.at[sent], here, device_id=to, device_id_type=MESH)
        cp.start()
        return cp

    def take(part, sem):
        pltpu.make_async_copy(part, part, sem).wait()

    zcp = [send(tks.at[0, q, k], tks.at[1, q, k], zmate, 2) for q in range(2)]
    for q in range(2):
        send(tks.at[0, q, k], tks.at[0, q, k], core, 3 + q, 2 + q)
    scp = []
    for d in range(1, PL):
        _, x_, c_ = mate(d)
        scp.append(send(pr.at[k], pr.at[k], dev(x_, h, c_), 1, 1))
    for dx, dc in ((0, 1), (1, 0), (3, 0), (2, 0), (1, 1), (3, 1), (2, 1)):
        x_, c_ = rem(x + dx, 4), rem(c + dc, 2)
        send(wdn.at[0, :, cols_of(x_ * 2 + c_, COLS)], wd.at[cols_of(k, FF1)], dev(x_, h, c_), 0, 0)

    col0, col1 = pl.ds(0, HALF), pl.ds(HALF, HALF)

    class Chunk:
        def __init__(self, plane, q):
            self.plane, self.q = plane, q
            self.t = tks.at[plane, q]

        def piece(self, slot, cols, to, got=None):
            part = self.t.at[slot, :, cols]
            return send(part, part, to, 3 + self.plane * 2 + self.q, got)

        def to_core(self, slot, cols):
            self.piece(slot, cols, core, 2 + self.plane * 2 + self.q)

        def first(self):
            if self.plane == 1:
                zcp[self.q].wait_recv()
            self.r0 = self.piece(k, col0, right)
            self.l1 = self.piece(k, col1, left)
            self.r1 = self.piece(k, col1, right)
            self.l0 = self.piece(k, col0, left)
            if self.plane == 1:
                self.to_core(k, pl.ds(0, D))

        def second(self):
            self.r0.wait_recv()
            self.f0 = self.piece(slot_l, col0, right)
            self.l1.wait_recv()
            self.f1 = self.piece(slot_r, col1, left)
            self.to_core(slot_l, col0)
            self.to_core(slot_r, col1)

        def finish(self):
            for cp, slot, cols in ((self.r1, slot_l, col1), (self.l0, slot_r, col0), (self.f0, slot_2, col0), (self.f1, slot_2, col1)):
                cp.wait_recv()
                self.to_core(slot, cols)
            take(self.t.at[pl.ds(0, 4)], bs.at[2 + self.plane * 2 + self.q])

        def gate_up(self):
            tk = self.t
            self.hid = hid.at[self.plane * 2 + self.q]
            both = jnp.dot(tk[...].reshape(ROWS, D), wgu[...], preferred_element_type=F32)
            gate = both[:, :FF1]
            self.hid[:, cols_of(k, FF1)] = (gate / (1.0 + jnp.exp(-gate)) * both[:, FF1:]).astype(BF)
            mine = self.hid.at[:, cols_of(k, FF1)]
            n = self.plane * 2 + self.q
            self.lane = [(send(mine, mine, to, 7 + n), slot) for to, slot in ((across, slot_2), (right, slot_l), (left, slot_r))]
            send(mine, mine, core, 7 + n, 6 + n)

        def collect(self):
            n = self.plane * 2 + self.q
            for cp, slot in self.lane[1:] + self.lane[:1]:
                cp.wait_recv()
                part = self.hid.at[:, cols_of(slot, FF1)]
                send(part, part, core, 7 + n, 6 + n)
            take(self.hid.at[:, pl.ds(0, 4 * FF1)], bs.at[6 + n])

        def down(self):
            for start, width in ((0, 256), (256, 256), (512, 256), (768, 128)):
                cols = pl.ds(start, width)
                value = jnp.dot(self.hid[...], wd[:, cols], preferred_element_type=F32).reshape(PL, HR, width)
                if self.plane == 1:
                    zs[self.q, :, :, cols] = value.astype(BF)
                else:
                    oacc[self.q, :, :, cols] = value
            if self.plane == 1:
                self.z = []
                for d in range(PL):
                    kk, _, _ = mate(d)
                    self.z.append(send(zs.at[self.q, kk], zr.at[self.q, kk], zmate, 11 + self.q))

    mycols = cols_of(k, COLS)

    def last_hop(q, ch):
        for d in range(PL):
            kk, x_, c_ = mate(d)
            ch.z[d].wait_recv()
            scale = sc[kk, pl.ds(q * HR, HR), :]
            for j in range(0, COLS, 128):
                cols = pl.ds(j, 128)
                total = (oacc[q, kk, :, cols] + zr[q, kk, :, cols].astype(F32)) * scale
                total = jnp.where(scale > 0.0, total, 0.0)
                fs[q, kk, :, :, cols] = total.reshape(8, 2, 128).astype(BF)
            for t in range(8):
                s = rem(e + t, 8)
                src, dst = fs.at[q, kk, s], out.at[0, pl.ds(4 * e + 2 * q, 2), mycols]
                sem = fss.at[q, 0] if d else fs0.at[q] if t == 0 else fss.at[q, 1]
                remote = pltpu.make_async_remote_copy(src, dst, sem, fsr, device_id=dev(x_, h, c_, s), device_id_type=MESH)
                if d == 0 and t == 0:
                    pl.when(e >= 8)(remote.start)
                    pl.when(e < 8)(pltpu.make_async_copy(src, dst, fsr).start)
                else:
                    remote.start()

    p0, p1, o0, o1 = Chunk(1, 0), Chunk(1, 1), Chunk(0, 0), Chunk(0, 1)
    @pl.when(e >= 8)
    def _():
        zero[...] = jnp.zeros_like(zero)
        for i in range(8):
            pltpu.make_async_copy(zero, out.at[0, pl.ds(8 * i, 8)], zsem).start()

    p0.first()
    p0.second()
    p1.first()
    loads[1].wait()
    loads[2].wait()
    p0.finish()
    p0.gate_up()
    p1.second()

    take(pr.at[pl.ds(0, 7)], bs.at[1])
    slot_i = lax.broadcasted_iota(jnp.int32, (2 * HR, 128), 1)
    row_i = lax.broadcasted_iota(jnp.int32, (2 * HR, 128), 0)
    from_i = 4 * div(rem(row_i, HR), 2) + 2 * div(row_i, HR) + rem(row_i, 2)
    for kk in range(PL):
        column = jnp.sum(jnp.where(slot_i == from_i, pr[kk], 0.0), axis=1, keepdims=True)
        sc[kk] = jnp.broadcast_to(column, (2 * HR, 128))
    o0.first()
    p0.collect()
    loads[3].wait()
    take(wd.at[pl.ds(0, 7 * FF1)], bs.at[0])
    p0.down()
    p1.finish()
    p1.gate_up()
    o0.second()
    o1.first()
    p1.collect()
    p1.down()
    o0.finish()
    o0.gate_up()
    o1.second()
    o0.collect()
    o0.down()
    o1.finish()
    o1.gate_up()
    last_hop(0, p0)
    o1.collect()
    o1.down()
    last_hop(1, p1)

    take(wd.at[pl.ds(0, 7 * FF1)], ss.at[0])
    take(pr.at[pl.ds(0, 7)], ss.at[1])
    take(tks.at[0, 0, pl.ds(0, 2)], ss.at[2])
    for n in range(4):
        take(tks.at[0, 0, pl.ds(0, 7)], ss.at[3 + n])
        take(hid.at[0, :, pl.ds(0, 7 * FF1)], ss.at[7 + n])
    for q in range(2):
        take(zs.at[q], ss.at[11 + q])
    for q in range(2):
        take(fs.at[q, pl.ds(0, PL - 1)], fss.at[q, 0])
        take(fs.at[q, 0, pl.ds(0, 7)], fss.at[q, 1])

        @pl.when(e >= 8)
        def _():
            take(fs.at[q, 0, 0], fs0.at[q])

    @pl.when(e >= 8)
    def _():
        take(out, zsem)

    @pl.when(e < 8)
    def _():
        take(out, fsr)


def body(tokens, route_prob, counts, w_gate, w_up, w_down):
    any_ = pl.BlockSpec(memory_space=pl.ANY)
    smem = pl.BlockSpec(memory_space=pltpu.SMEM)
    out = pl.pallas_call(
        kernel,
        name="routed_experts",
        out_shape=jax.ShapeDtypeStruct((1, 64, D), BF),
        in_specs=[smem, pl.BlockSpec(memory_space=pltpu.VMEM), any_, any_, any_, any_],
        out_specs=any_,
        scratch_shapes=[
            pltpu.VMEM((D, 2 * FF1), BF),
            pltpu.VMEM((PL * FF1, COLS), BF),
            pltpu.VMEM((2 * HR, D), BF),
            pltpu.VMEM((2, 2, PL, HR, D), BF),
            pltpu.VMEM((4, ROWS, PL * FF1), BF),
            pltpu.VMEM((2, PL, HR, COLS), BF),
            pltpu.VMEM((2, PL, HR, COLS), BF),
            pltpu.VMEM((2, PL, HR, COLS), F32),
            pltpu.VMEM((2, PL, 8, 2, COLS), BF),
            pltpu.VMEM((PL, 1, 128), F32),
            pltpu.VMEM((PL, 2 * HR, 128), F32),
            pltpu.VMEM((8, D), BF),
            pltpu.SemaphoreType.DMA((13,)),
            pltpu.SemaphoreType.DMA((54,)),
            pltpu.SemaphoreType.DMA((10,)),
            pltpu.SemaphoreType.DMA((4,)),
            pltpu.SemaphoreType.DMA((2, 2)),
            pltpu.SemaphoreType.DMA,
            pltpu.SemaphoreType.DMA((2,)),
            pltpu.SemaphoreType.DMA,
        ],
        compiler_params=pltpu.CompilerParams(
            collective_id=0, has_side_effects=True, vmem_limit_bytes=60 * 1024 * 1024),
    )(counts, route_prob, tokens, w_gate, w_up, w_down)
    return out


def solution(mesh):
    in_specs = (
        P("expert", "batch", None),
        P("expert", "batch"),
        P(),
        P("expert", None, "batch"),
        P("expert", None, "batch"),
        P("expert", "batch", None),
    )
    out_specs = P("expert", "batch", None)
    return jax.shard_map(body, mesh=mesh, in_specs=in_specs, out_specs=out_specs, check_vma=False)
```

```python
import jax
import jax.numpy as jnp
from jax import lax
from jax.experimental import pallas as pl
from jax.experimental.pallas import tpu as pltpu
from jax.sharding import PartitionSpec as P

MESH = pl.DeviceIdType.MESH
BF = jnp.bfloat16
F32 = jnp.float32

D = 7168
RING = 2560
FF1 = 128
PL = 8
COLS = D // PL
HR = 16
ROWS = PL * HR
KSTEP = 1024


def kernel(counts, prob, tok, wg, wu, wdn, out, wgu, wd, raw, tks, hid, zs, zr, oacc, fs, pr, sc, zero, ss, rs, bs, ls, fss, fsr, fs0, zsem):
    div, rem = lax.div, lax.rem
    e = lax.axis_index("expert")
    b = lax.axis_index("batch")
    x, h, c = div(b, 4), rem(div(b, 2), 2), rem(b, 2)
    k = x * 2 + c
    xr, x2, xl = rem(x + 1, 4), rem(x + 2, 4), rem(x + 3, 4)

    def dev(x_, h_, c_, e_=e):
        return (e_, x_ * 4 + h_ * 2 + c_)

    def mate(d):
        kk = rem(k + d, PL)
        return kk, div(kk, 2), rem(kk, 2)

    right, left, across = dev(xr, h, c), dev(xl, h, c), dev(x2, h, c)
    core, zmate = dev(x, h, 1 - c), dev(x, 1 - h, c)
    slot_r, slot_2, slot_l = xr * 2 + c, x2 * 2 + c, xl * 2 + c

    def cols_of(kk, width):
        return pl.ds(pl.multiple_of(kk * width, 128), width)

    loads = [
        pltpu.make_async_copy(tok.at[0, pl.ds(0, 2 * HR)], raw, ls.at[3]),
        pltpu.make_async_copy(wg.at[0], wgu.at[:, pl.ds(0, FF1)], ls.at[0]),
        pltpu.make_async_copy(wu.at[0], wgu.at[:, pl.ds(FF1, FF1)], ls.at[1]),
        pltpu.make_async_copy(wdn.at[0, :, cols_of(k, COLS)], wd.at[cols_of(k, FF1)], ls.at[2]),
    ]
    for cp in loads:
        cp.start()

    bar = pltpu.get_barrier_semaphore()

    def greet(to):
        pl.semaphore_signal(bar, inc=1, device_id=to, device_id_type=MESH)

    for d in range(1, PL):
        _, x_, c_ = mate(d)
        greet(dev(x_, h, c_))
    greet(zmate)

    @pl.when(e < 8)
    def _():
        for t in range(16):
            for d in range(PL):
                _, x_, c_ = mate(d)
                greet(dev(x_, h, c_, rem(e + t, 16)))

    loads[0].wait()
    new = lax.broadcasted_iota(jnp.int32, (2 * HR, 2 * HR), 0)
    old = lax.broadcasted_iota(jnp.int32, (2 * HR, 2 * HR), 1)
    source = 4 * div(rem(new, HR), 2) + 2 * div(new, HR) + rem(new, 2)
    order = jnp.where(source == old, 1.0, 0.0).astype(BF)

    def reorder(i, _):
        cols = pl.ds(pl.multiple_of(i * KSTEP, KSTEP), KSTEP)
        value = jnp.dot(order, raw[:, cols], preferred_element_type=F32).astype(BF)
        tks[0, 0, k, :, cols] = value[:HR]
        tks[0, 1, k, :, cols] = value[HR:]
        return 0

    lax.fori_loop(0, D // KSTEP, reorder, 0)

    own = counts[e, b]
    slots = lax.broadcasted_iota(jnp.int32, (1, 64), 1)
    pr[k] = jnp.zeros((1, 128), F32)
    pr[k, :, pl.ds(0, 64)] = jnp.where(slots < own, prob[...], 0.0)

    pl.semaphore_wait(bar, PL + 64)

    count = []

    def send(src, dst, to, sent, got=None):
        if got is None:
            here = rs.at[len(count)]
            count.append(0)
        else:
            here = bs.at[got]
        cp = pltpu.make_async_remote_copy(src, dst, ss.at[sent], here, device_id=to, device_id_type=MESH)
        cp.start()
        return cp

    def take(part, sem):
        pltpu.make_async_copy(part, part, sem).wait()

    zcp = [send(tks.at[0, q, k], tks.at[1, q, k], zmate, 2) for q in range(2)]
    for q in range(2):
        send(tks.at[0, q, k], tks.at[0, q, k], core, 3 + q, 2 + q)
    scp = []
    for d in range(1, PL):
        _, x_, c_ = mate(d)
        scp.append(send(pr.at[k], pr.at[k], dev(x_, h, c_), 1, 1))
    for dx, dc in ((0, 1), (1, 0), (3, 0), (2, 0), (1, 1), (3, 1), (2, 1)):
        x_, c_ = rem(x + dx, 4), rem(c + dc, 2)
        send(wdn.at[0, :, cols_of(x_ * 2 + c_, COLS)], wd.at[cols_of(k, FF1)], dev(x_, h, c_), 0, 0)

    rest = pl.ds(2 * RING, D - 2 * RING)

    class Chunk:
        def __init__(self, plane, q):
            self.plane, self.q = plane, q
            self.t = tks.at[plane, q]
            self.ring = RING if plane == 0 and q == 0 else D // 2
            self.col0, self.col1 = pl.ds(0, self.ring), pl.ds(self.ring, self.ring)

        def piece(self, slot, cols, to, got=None):
            part = self.t.at[slot, :, cols]
            return send(part, part, to, 3 + self.plane * 2 + self.q, got)

        def to_core(self, slot, cols):
            self.piece(slot, cols, core, 2 + self.plane * 2 + self.q)

        def first(self):
            if self.plane == 1:
                zcp[self.q].wait_recv()
            self.r0 = self.piece(k, self.col0, right)
            self.l1 = self.piece(k, self.col1, left)
            self.r1 = self.piece(k, self.col1, right)
            self.l0 = self.piece(k, self.col0, left)
            if self.plane == 1:
                self.to_core(k, pl.ds(0, D))

        def second(self):
            self.r0.wait_recv()
            self.f0 = self.piece(slot_l, self.col0, right)
            self.l1.wait_recv()
            self.f1 = self.piece(slot_r, self.col1, left)
            self.to_core(slot_l, self.col0)
            self.to_core(slot_r, self.col1)

        def finish(self, meanwhile=None):
            for cp, slot, cols in ((self.r1, slot_l, self.col1), (self.l0, slot_r, self.col0), (self.f0, slot_2, self.col0), (self.f1, slot_2, self.col1)):
                cp.wait_recv()
                self.to_core(slot, cols)
            if self.q == 0 and self.plane == 1:
                self.along_z = [
                    (send(self.t.at[slot, :, rest], tks.at[0, 0, slot, :, rest], zmate, 13), slot)
                    for slot in (slot_l, slot_r, slot_2)]
            if self.q == 0 and self.plane == 0:
                for cp, slot in p0.along_z:
                    cp.wait_recv()
                    part = self.t.at[slot, :, rest]
                    send(part, part, core, 13, 2)
            if meanwhile is not None:
                meanwhile()
            take(self.t.at[pl.ds(0, 4)], bs.at[2 + self.plane * 2 + self.q])

        def gate_up(self):
            tk = self.t
            self.hid = hid.at[self.plane * 2 + self.q]
            both = jnp.dot(tk[...].reshape(ROWS, D), wgu[...], preferred_element_type=F32)
            gate = both[:, :FF1]
            self.hid[:, cols_of(k, FF1)] = (gate / (1.0 + jnp.exp(-gate)) * both[:, FF1:]).astype(BF)
            mine = self.hid.at[:, cols_of(k, FF1)]
            n = self.plane * 2 + self.q
            self.lane = [(send(mine, mine, to, 7 + n), slot) for to, slot in ((across, slot_2), (right, slot_l), (left, slot_r))]
            send(mine, mine, core, 7 + n, 6 + n)

        def collect(self):
            n = self.plane * 2 + self.q
            for cp, slot in self.lane[1:] + self.lane[:1]:
                cp.wait_recv()
                part = self.hid.at[:, cols_of(slot, FF1)]
                send(part, part, core, 7 + n, 6 + n)
            take(self.hid.at[:, pl.ds(0, 4 * FF1)], bs.at[6 + n])

        def down(self):
            for start, width in ((0, 256), (256, 256), (512, 256), (768, 128)):
                cols = pl.ds(start, width)
                value = jnp.dot(self.hid[...], wd[:, cols], preferred_element_type=F32).reshape(PL, HR, width)
                if self.plane == 1:
                    zs[self.q, :, :, cols] = value.astype(BF)
                else:
                    oacc[self.q, :, :, cols] = value
            if self.plane == 1:
                self.z = []
                for d in range(PL):
                    kk, _, _ = mate(d)
                    self.z.append(send(zs.at[self.q, kk], zr.at[self.q, kk], zmate, 11 + self.q))

    mycols = cols_of(k, COLS)

    def last_hop(q, ch):
        for d in range(PL):
            kk, x_, c_ = mate(d)
            ch.z[d].wait_recv()
            scale = sc[kk, pl.ds(q * HR, HR), :]
            for j in range(0, COLS, 128):
                cols = pl.ds(j, 128)
                total = (oacc[q, kk, :, cols] + zr[q, kk, :, cols].astype(F32)) * scale
                total = jnp.where(scale > 0.0, total, 0.0)
                fs[q, kk, :, :, cols] = total.reshape(8, 2, 128).astype(BF)
            for t in range(8):
                s = rem(e + t, 8)
                src, dst = fs.at[q, kk, s], out.at[0, pl.ds(4 * e + 2 * q, 2), mycols]
                sem = fss.at[q, 0] if d else fs0.at[q] if t == 0 else fss.at[q, 1]
                remote = pltpu.make_async_remote_copy(src, dst, sem, fsr, device_id=dev(x_, h, c_, s), device_id_type=MESH)
                if d == 0 and t == 0:
                    pl.when(e >= 8)(remote.start)
                    pl.when(e < 8)(pltpu.make_async_copy(src, dst, fsr).start)
                else:
                    remote.start()

    p0, p1, o0, o1 = Chunk(1, 0), Chunk(1, 1), Chunk(0, 0), Chunk(0, 1)
    @pl.when(e >= 8)
    def _():
        zero[...] = jnp.zeros_like(zero)
        for i in range(8):
            pltpu.make_async_copy(zero, out.at[0, pl.ds(8 * i, 8)], zsem).start()

    p0.first()
    p0.second()
    p1.first()
    loads[1].wait()
    loads[2].wait()
    p0.finish()
    p0.gate_up()
    p1.second()

    take(pr.at[pl.ds(0, 7)], bs.at[1])
    slot_i = lax.broadcasted_iota(jnp.int32, (2 * HR, 128), 1)
    row_i = lax.broadcasted_iota(jnp.int32, (2 * HR, 128), 0)
    from_i = 4 * div(rem(row_i, HR), 2) + 2 * div(row_i, HR) + rem(row_i, 2)
    for kk in range(PL):
        column = jnp.sum(jnp.where(slot_i == from_i, pr[kk], 0.0), axis=1, keepdims=True)
        sc[kk] = jnp.broadcast_to(column, (2 * HR, 128))
    o0.first()
    p0.collect()
    loads[3].wait()
    take(wd.at[pl.ds(0, 7 * FF1)], bs.at[0])
    p0.down()
    p1.finish()
    p1.gate_up()
    o0.second()
    o1.first()
    p1.collect()
    p1.down()
    o0.finish()
    o0.gate_up()
    o1.second()
    o0.collect()
    o0.down()
    o1.finish(lambda: last_hop(0, p0))
    o1.gate_up()
    o1.collect()
    o1.down()
    last_hop(1, p1)

    take(wd.at[pl.ds(0, 7 * FF1)], ss.at[0])
    take(pr.at[pl.ds(0, 7)], ss.at[1])
    take(tks.at[0, 0, pl.ds(0, 2)], ss.at[2])
    take(tks.at[0, 0, pl.ds(0, 6), :, pl.ds(0, D - 2 * RING)], ss.at[13])
    for n in range(4):
        if n == 0:
            take(tks.at[0, 0, :, :, pl.ds(0, (12 * RING + D) // PL)], ss.at[3])
        else:
            take(tks.at[0, 0, pl.ds(0, 7)], ss.at[3 + n])
        take(hid.at[0, :, pl.ds(0, 7 * FF1)], ss.at[7 + n])
    for q in range(2):
        take(zs.at[q], ss.at[11 + q])
    for q in range(2):
        take(fs.at[q, pl.ds(0, PL - 1)], fss.at[q, 0])
        take(fs.at[q, 0, pl.ds(0, 7)], fss.at[q, 1])

        @pl.when(e >= 8)
        def _():
            take(fs.at[q, 0, 0], fs0.at[q])

    @pl.when(e >= 8)
    def _():
        take(out, zsem)

    @pl.when(e < 8)
    def _():
        take(out, fsr)


def body(tokens, route_prob, counts, w_gate, w_up, w_down):
    any_ = pl.BlockSpec(memory_space=pl.ANY)
    smem = pl.BlockSpec(memory_space=pltpu.SMEM)
    out = pl.pallas_call(
        kernel,
        name="routed_experts",
        out_shape=jax.ShapeDtypeStruct((1, 64, D), BF),
        in_specs=[smem, pl.BlockSpec(memory_space=pltpu.VMEM), any_, any_, any_, any_],
        out_specs=any_,
        scratch_shapes=[
            pltpu.VMEM((D, 2 * FF1), BF),
            pltpu.VMEM((PL * FF1, COLS), BF),
            pltpu.VMEM((2 * HR, D), BF),
            pltpu.VMEM((2, 2, PL, HR, D), BF),
            pltpu.VMEM((4, ROWS, PL * FF1), BF),
            pltpu.VMEM((2, PL, HR, COLS), BF),
            pltpu.VMEM((2, PL, HR, COLS), BF),
            pltpu.VMEM((2, PL, HR, COLS), F32),
            pltpu.VMEM((2, PL, 8, 2, COLS), BF),
            pltpu.VMEM((PL, 1, 128), F32),
            pltpu.VMEM((PL, 2 * HR, 128), F32),
            pltpu.VMEM((8, D), BF),
            pltpu.SemaphoreType.DMA((14,)),
            pltpu.SemaphoreType.DMA((57,)),
            pltpu.SemaphoreType.DMA((10,)),
            pltpu.SemaphoreType.DMA((4,)),
            pltpu.SemaphoreType.DMA((2, 2)),
            pltpu.SemaphoreType.DMA,
            pltpu.SemaphoreType.DMA((2,)),
            pltpu.SemaphoreType.DMA,
        ],
        compiler_params=pltpu.CompilerParams(
            collective_id=0, has_side_effects=True, vmem_limit_bytes=60 * 1024 * 1024),
    )(counts, route_prob, tokens, w_gate, w_up, w_down)
    return out


def solution(mesh):
    in_specs = (
        P("expert", "batch", None),
        P("expert", "batch"),
        P(),
        P("expert", None, "batch"),
        P("expert", None, "batch"),
        P("expert", "batch", None),
    )
    out_specs = P("expert", "batch", None)
    return jax.shard_map(body, mesh=mesh, in_specs=in_specs, out_specs=out_specs, check_vma=False)
```

```python
import jax
import jax.numpy as jnp
from jax import lax
from jax.experimental import pallas as pl
from jax.experimental.pallas import tpu as pltpu
from jax.sharding import PartitionSpec as P

MESH = pl.DeviceIdType.MESH
BF = jnp.bfloat16
F32 = jnp.float32

D = 7168
RING = 2560
FF1 = 128
PL = 8
COLS = D // PL
HR = 16
ROWS = PL * HR
KSTEP = 1024


def kernel(counts, prob, tok, wg, wu, wdn, out, wgu, wd, raw, tks, hid, zs, zr, oacc, fs, pr, sc, zero, ss, rs, bs, ls, fss, fsr, fs0, zsem):
    div, rem = lax.div, lax.rem
    e = lax.axis_index("expert")
    b = lax.axis_index("batch")
    x, h, c = div(b, 4), rem(div(b, 2), 2), rem(b, 2)
    k = x * 2 + c
    xr, x2, xl = rem(x + 1, 4), rem(x + 2, 4), rem(x + 3, 4)

    def dev(x_, h_, c_, e_=e):
        return (e_, x_ * 4 + h_ * 2 + c_)

    def mate(d):
        kk = rem(k + d, PL)
        return kk, div(kk, 2), rem(kk, 2)

    right, left, across = dev(xr, h, c), dev(xl, h, c), dev(x2, h, c)
    core, zmate = dev(x, h, 1 - c), dev(x, 1 - h, c)
    slot_r, slot_2, slot_l = xr * 2 + c, x2 * 2 + c, xl * 2 + c

    def cols_of(kk, width):
        return pl.ds(pl.multiple_of(kk * width, 128), width)

    loads = [
        pltpu.make_async_copy(tok.at[0, pl.ds(0, 2 * HR)], raw, ls.at[3]),
        pltpu.make_async_copy(wg.at[0], wgu.at[:, pl.ds(0, FF1)], ls.at[0]),
        pltpu.make_async_copy(wu.at[0], wgu.at[:, pl.ds(FF1, FF1)], ls.at[1]),
        pltpu.make_async_copy(wdn.at[0, :, cols_of(k, COLS)], wd.at[cols_of(k, FF1)], ls.at[2]),
    ]
    for cp in loads:
        cp.start()

    bar = pltpu.get_barrier_semaphore()

    def greet(to):
        pl.semaphore_signal(bar, inc=1, device_id=to, device_id_type=MESH)

    for d in range(1, PL):
        _, x_, c_ = mate(d)
        greet(dev(x_, h, c_))
    greet(zmate)

    @pl.when(e < 8)
    def _():
        for t in range(16):
            for d in range(PL):
                _, x_, c_ = mate(d)
                greet(dev(x_, h, c_, rem(e + t, 16)))

    loads[0].wait()
    new = lax.broadcasted_iota(jnp.int32, (2 * HR, 2 * HR), 0)
    old = lax.broadcasted_iota(jnp.int32, (2 * HR, 2 * HR), 1)
    source = 4 * div(rem(new, HR), 2) + 2 * div(new, HR) + rem(new, 2)
    order = jnp.where(source == old, 1.0, 0.0).astype(BF)

    def reorder(i, _):
        cols = pl.ds(pl.multiple_of(i * KSTEP, KSTEP), KSTEP)
        value = jnp.dot(order, raw[:, cols], preferred_element_type=F32).astype(BF)
        tks[0, 0, k, :, cols] = value[:HR]
        tks[0, 1, k, :, cols] = value[HR:]
        return 0

    lax.fori_loop(0, D // KSTEP, reorder, 0)

    own = counts[e, b]
    slots = lax.broadcasted_iota(jnp.int32, (1, 64), 1)
    pr[k] = jnp.zeros((1, 128), F32)
    pr[k, :, pl.ds(0, 64)] = jnp.where(slots < own, prob[...], 0.0)

    pl.semaphore_wait(bar, PL + 64)

    count = []

    def send(src, dst, to, sent, got=None):
        if got is None:
            here = rs.at[len(count)]
            count.append(0)
        else:
            here = bs.at[got]
        cp = pltpu.make_async_remote_copy(src, dst, ss.at[sent], here, device_id=to, device_id_type=MESH)
        cp.start()
        return cp

    def take(part, sem):
        pltpu.make_async_copy(part, part, sem).wait()

    zcp = [send(tks.at[0, q, k], tks.at[1, q, k], zmate, 2) for q in range(2)]
    for q in range(2):
        send(tks.at[0, q, k], tks.at[0, q, k], core, 3 + q, 2 + q)
    scp = []
    for d in range(1, PL):
        _, x_, c_ = mate(d)
        scp.append(send(pr.at[k], pr.at[k], dev(x_, h, c_), 1, 1))
    for dx, dc in ((2, 0), (2, 1), (1, 0), (3, 0), (1, 1), (3, 1), (0, 1)):
        x_, c_ = rem(x + dx, 4), rem(c + dc, 2)
        send(wdn.at[0, :, cols_of(x_ * 2 + c_, COLS)], wd.at[cols_of(k, FF1)], dev(x_, h, c_), 0, 0)

    rest = pl.ds(2 * RING, D - 2 * RING)

    class Chunk:
        def __init__(self, plane, q):
            self.plane, self.q = plane, q
            self.t = tks.at[plane, q]
            self.ring = RING if plane == 0 and q == 0 else D // 2
            self.col0, self.col1 = pl.ds(0, self.ring), pl.ds(self.ring, self.ring)

        def piece(self, slot, cols, to, got=None):
            part = self.t.at[slot, :, cols]
            return send(part, part, to, 3 + self.plane * 2 + self.q, got)

        def to_core(self, slot, cols):
            self.piece(slot, cols, core, 2 + self.plane * 2 + self.q)

        def first(self):
            if self.plane == 1:
                zcp[self.q].wait_recv()
            self.r0 = self.piece(k, self.col0, right)
            self.l1 = self.piece(k, self.col1, left)
            self.r1 = self.piece(k, self.col1, right)
            self.l0 = self.piece(k, self.col0, left)
            if self.plane == 1:
                self.to_core(k, pl.ds(0, D))

        def second(self):
            self.r0.wait_recv()
            self.f0 = self.piece(slot_l, self.col0, right)
            self.l1.wait_recv()
            self.f1 = self.piece(slot_r, self.col1, left)
            self.to_core(slot_l, self.col0)
            self.to_core(slot_r, self.col1)

        def finish(self, meanwhile=None):
            for cp, slot, cols in ((self.r1, slot_l, self.col1), (self.l0, slot_r, self.col0), (self.f0, slot_2, self.col0), (self.f1, slot_2, self.col1)):
                cp.wait_recv()
                self.to_core(slot, cols)
            if self.q == 0 and self.plane == 1:
                self.along_z = [
                    (send(self.t.at[slot, :, rest], tks.at[0, 0, slot, :, rest], zmate, 13), slot)
                    for slot in (slot_l, slot_r, slot_2)]
            if self.q == 0 and self.plane == 0:
                for cp, slot in p0.along_z:
                    cp.wait_recv()
                    part = self.t.at[slot, :, rest]
                    send(part, part, core, 13, 2)
            if meanwhile is not None:
                meanwhile()
            take(self.t.at[pl.ds(0, 4)], bs.at[2 + self.plane * 2 + self.q])

        def gate_up(self):
            tk = self.t
            self.hid = hid.at[self.plane * 2 + self.q]
            both = jnp.dot(tk[...].reshape(ROWS, D), wgu[...], preferred_element_type=F32)
            gate = both[:, :FF1]
            self.hid[:, cols_of(k, FF1)] = (gate / (1.0 + jnp.exp(-gate)) * both[:, FF1:]).astype(BF)
            mine = self.hid.at[:, cols_of(k, FF1)]
            n = self.plane * 2 + self.q
            self.lane = [(send(mine, mine, to, 7 + n), slot) for to, slot in ((across, slot_2), (right, slot_l), (left, slot_r))]
            send(mine, mine, core, 7 + n, 6 + n)

        def collect(self):
            n = self.plane * 2 + self.q
            for cp, slot in self.lane[1:] + self.lane[:1]:
                cp.wait_recv()
                part = self.hid.at[:, cols_of(slot, FF1)]
                send(part, part, core, 7 + n, 6 + n)
            take(self.hid.at[:, pl.ds(0, 4 * FF1)], bs.at[6 + n])

        def down(self):
            for start, width in ((0, 256), (256, 256), (512, 256), (768, 128)):
                cols = pl.ds(start, width)
                value = jnp.dot(self.hid[...], wd[:, cols], preferred_element_type=F32).reshape(PL, HR, width)
                if self.plane == 1:
                    zs[self.q, :, :, cols] = value.astype(BF)
                else:
                    oacc[self.q, :, :, cols] = value
            if self.plane == 1:
                self.z = []
                for d in range(PL):
                    kk, _, _ = mate(d)
                    self.z.append(send(zs.at[self.q, kk], zr.at[self.q, kk], zmate, 11 + self.q))

    mycols = cols_of(k, COLS)

    def last_hop(q, ch):
        for d in (4, 3, 5, 2, 6, 1, 7, 0):
            kk, x_, c_ = mate(d)
            ch.z[d].wait_recv()
            scale = sc[kk, pl.ds(q * HR, HR), :]
            for j in range(0, COLS, 128):
                cols = pl.ds(j, 128)
                total = (oacc[q, kk, :, cols] + zr[q, kk, :, cols].astype(F32)) * scale
                total = jnp.where(scale > 0.0, total, 0.0)
                fs[q, kk, :, :, cols] = total.reshape(8, 2, 128).astype(BF)
            for t in (2, 6, 3, 7, 1, 5, 4, 0):
                s = rem(e + t, 8)
                src, dst = fs.at[q, kk, s], out.at[0, pl.ds(4 * e + 2 * q, 2), mycols]
                sem = fss.at[q, 0] if d else fs0.at[q] if t == 0 else fss.at[q, 1]
                remote = pltpu.make_async_remote_copy(src, dst, sem, fsr, device_id=dev(x_, h, c_, s), device_id_type=MESH)
                if d == 0 and t == 0:
                    pl.when(e >= 8)(remote.start)
                    pl.when(e < 8)(pltpu.make_async_copy(src, dst, fsr).start)
                else:
                    remote.start()

    p0, p1, o0, o1 = Chunk(1, 0), Chunk(1, 1), Chunk(0, 0), Chunk(0, 1)
    @pl.when(e >= 8)
    def _():
        zero[...] = jnp.zeros_like(zero)
        for i in range(8):
            pltpu.make_async_copy(zero, out.at[0, pl.ds(8 * i, 8)], zsem).start()

    p0.first()
    p0.second()
    p1.first()
    loads[1].wait()
    loads[2].wait()
    p0.finish()
    p0.gate_up()
    p1.second()

    take(pr.at[pl.ds(0, 7)], bs.at[1])
    slot_i = lax.broadcasted_iota(jnp.int32, (2 * HR, 128), 1)
    row_i = lax.broadcasted_iota(jnp.int32, (2 * HR, 128), 0)
    from_i = 4 * div(rem(row_i, HR), 2) + 2 * div(row_i, HR) + rem(row_i, 2)
    for kk in range(PL):
        column = jnp.sum(jnp.where(slot_i == from_i, pr[kk], 0.0), axis=1, keepdims=True)
        sc[kk] = jnp.broadcast_to(column, (2 * HR, 128))
    o0.first()
    p0.collect()
    loads[3].wait()
    take(wd.at[pl.ds(0, 7 * FF1)], bs.at[0])
    p0.down()
    p1.finish()
    p1.gate_up()
    o0.second()
    o1.first()
    p1.collect()
    p1.down()
    o0.finish()
    o0.gate_up()
    o1.second()
    o0.collect()
    o0.down()
    o1.finish(lambda: last_hop(0, p0))
    o1.gate_up()
    o1.collect()
    o1.down()
    last_hop(1, p1)

    take(wd.at[pl.ds(0, 7 * FF1)], ss.at[0])
    take(pr.at[pl.ds(0, 7)], ss.at[1])
    take(tks.at[0, 0, pl.ds(0, 2)], ss.at[2])
    take(tks.at[0, 0, pl.ds(0, 6), :, pl.ds(0, D - 2 * RING)], ss.at[13])
    for n in range(4):
        if n == 0:
            take(tks.at[0, 0, :, :, pl.ds(0, (12 * RING + D) // PL)], ss.at[3])
        else:
            take(tks.at[0, 0, pl.ds(0, 7)], ss.at[3 + n])
        take(hid.at[0, :, pl.ds(0, 7 * FF1)], ss.at[7 + n])
    for q in range(2):
        take(zs.at[q], ss.at[11 + q])
    for q in range(2):
        take(fs.at[q, pl.ds(0, PL - 1)], fss.at[q, 0])
        take(fs.at[q, 0, pl.ds(0, 7)], fss.at[q, 1])

        @pl.when(e >= 8)
        def _():
            take(fs.at[q, 0, 0], fs0.at[q])

    @pl.when(e >= 8)
    def _():
        take(out, zsem)

    @pl.when(e < 8)
    def _():
        take(out, fsr)


def body(tokens, route_prob, counts, w_gate, w_up, w_down):
    any_ = pl.BlockSpec(memory_space=pl.ANY)
    smem = pl.BlockSpec(memory_space=pltpu.SMEM)
    out = pl.pallas_call(
        kernel,
        name="routed_experts",
        out_shape=jax.ShapeDtypeStruct((1, 64, D), BF),
        in_specs=[smem, pl.BlockSpec(memory_space=pltpu.VMEM), any_, any_, any_, any_],
        out_specs=any_,
        scratch_shapes=[
            pltpu.VMEM((D, 2 * FF1), BF),
            pltpu.VMEM((PL * FF1, COLS), BF),
            pltpu.VMEM((2 * HR, D), BF),
            pltpu.VMEM((2, 2, PL, HR, D), BF),
            pltpu.VMEM((4, ROWS, PL * FF1), BF),
            pltpu.VMEM((2, PL, HR, COLS), BF),
            pltpu.VMEM((2, PL, HR, COLS), BF),
            pltpu.VMEM((2, PL, HR, COLS), F32),
            pltpu.VMEM((2, PL, 8, 2, COLS), BF),
            pltpu.VMEM((PL, 1, 128), F32),
            pltpu.VMEM((PL, 2 * HR, 128), F32),
            pltpu.VMEM((8, D), BF),
            pltpu.SemaphoreType.DMA((14,)),
            pltpu.SemaphoreType.DMA((57,)),
            pltpu.SemaphoreType.DMA((10,)),
            pltpu.SemaphoreType.DMA((4,)),
            pltpu.SemaphoreType.DMA((2, 2)),
            pltpu.SemaphoreType.DMA,
            pltpu.SemaphoreType.DMA((2,)),
            pltpu.SemaphoreType.DMA,
        ],
        compiler_params=pltpu.CompilerParams(
            collective_id=0, has_side_effects=True, vmem_limit_bytes=60 * 1024 * 1024),
    )(counts, route_prob, tokens, w_gate, w_up, w_down)
    return out


def solution(mesh):
    in_specs = (
        P("expert", "batch", None),
        P("expert", "batch"),
        P(),
        P("expert", None, "batch"),
        P("expert", None, "batch"),
        P("expert", "batch", None),
    )
    out_specs = P("expert", "batch", None)
    return jax.shard_map(body, mesh=mesh, in_specs=in_specs, out_specs=out_specs, check_vma=False)
```
